32 devices in a mesh: row: 8 (over z, y), col: 4 (over x, core).
Axes of the slice: x: 2, y: 2, z: 4, core: 2. Of those that a mesh axis runs over, the one named last changes fastest.
Arguments:
- saved_inputs: bfloat16 [8192, 4096], P(('row', 'col')), may hold values from -6 to 6
- output_grads: bfloat16 [8192, 14336], P(('row', 'col')), may hold values from -0.5 to 0.5
- proj_in: bfloat16 [4096, 128], replicated, may hold values from -0.09375 to 0.09375
- proj_out: bfloat16 [14336, 128], replicated, may hold values from -0.046875 to 0.046875
- doc_lengths: int32 [32], replicated, may hold values from 64 to 448, as said below
- device_docs: int32 [32], replicated, may hold values from 0 to 31, as said below
- fisher_inverse: float32 [16384, 16384], P('row', 'col'), may hold values from -0.3 to 2.3, as said below
Outputs:
- preconditioned: float32 [32, 16384], P('row', 'col')
The draws below stay inside these ranges and needn't reach their ends.
Inputs may be any that keep to these rules, and one draw needn't show every extreme that they name: `doc_lengths`: the lengths sum to 8192; some document has exactly 448 tokens and some exactly 64. `device_docs`: A permutation of the documents. `fisher_inverse`: Symmetric.
All inputs are finite; a program needn't handle non-finite values.
Results may differ from the reference program's by a relative error of at most 0.0041.
Values sent between devices are 32-bit elements; how exact they have to be, the bound alone decides.
No kernel may reach another device: no remote copies, remote signals or barrier semaphores. Data moves between devices by JAX's collectives and lax.ppermute only.
A program may use at most 128 MiB of HBM per device.

```python
import math
import jax
import jax.numpy as jnp
from jax import lax

D = 4096
FF = 14336
RANK_IN = 128
RANK_OUT = 128
TOK_DEV = 256
NFEAT = 16384
TOKENS = 8192
NDOC = 32
MEANLEN = 256
SPREAD = 192
MINLEN = 64


def draw_doc_lengths(key, part):
    key_extra, key_pick = jax.random.split(jax.random.fold_in(key, 11))
    extra = jax.random.randint(key_extra, (NDOC,), 0, SPREAD + 1)
    start_doc = jax.random.randint(key_pick, (), 1, NDOC - 8)
    index = jnp.arange(NDOC)
    fixed_points = (index == 0) | (index == start_doc - 1) | (index == start_doc + 9)
    extra = jnp.where(fixed_points, 0, extra)
    lengths = MEANLEN + extra - jnp.roll(extra, -1)
    planted = jnp.array([MINLEN, SPREAD + 1, MINLEN, MINLEN, MINLEN, MEANLEN + SPREAD, MEANLEN + SPREAD, MEANLEN + SPREAD, MEANLEN + SPREAD, MEANLEN + MINLEN - 1], dtype=jnp.int32)
    offset = index - (start_doc - 1)
    inside = (offset >= 0) & (offset < 10)
    lengths = jnp.where(inside, planted[jnp.clip(offset, 0, 9)], lengths)
    return lengths.astype(jnp.int32)


def draw_device_docs(key, part):
    first = jax.random.randint(jax.random.fold_in(key, 31), (), 0, NDOC)
    second = (first + 1) % NDOC
    third = (first + 1 + NDOC // 2) % NDOC
    index = jnp.arange(NDOC, dtype=jnp.int32)
    owners = jnp.where(index == first, second, jnp.where(index == second, third, jnp.where(index == third, first, index)))
    return owners.astype(jnp.int32)


def draw_fisher_inverse(key, part):
    key_noise, key_diag = jax.random.split(jax.random.fold_in(key, 23))
    noise = jnp.clip(jax.random.normal(key_noise, (NFEAT, NFEAT), jnp.float32), -4.0, 4.0)
    off_diag = 0.5 * (noise + noise.T) / math.sqrt(2.0 * NFEAT)
    diag_vals = jnp.exp(jax.random.uniform(key_diag, (NFEAT,), jnp.float32, math.log(0.5), math.log(2.0)))
    return (off_diag + jnp.diag(diag_vals)).astype(jnp.float32)


def level_of(key, dims, cuts, least, largest):
    def one(axis_at, parts):
        draws = jax.random.uniform(jax.random.fold_in(jax.random.fold_in(key, 6), axis_at), (parts,), jnp.float32, least / len(cuts), largest / len(cuts))
        return jnp.repeat(jnp.exp(draws), dims[axis_at] // parts).reshape((-1,) + (1,) * (len(dims) - axis_at - 1))

    gain = one(*cuts[0])
    for cut in cuts[1:]:
        gain = gain * one(*cut)
    return gain


def bell_draw(stream_key, dims, width, bound, cuts=(), held_as=jnp.bfloat16):
    drawn = width * jax.random.normal(stream_key, dims, jnp.float32)
    if cuts:
        drawn = drawn * level_of(stream_key, dims, cuts, -0.22, 0.18)
    return jnp.clip(drawn, -bound, bound).astype(held_as)


def setup_inputs(seed: int = 0) -> dict:
    key_list = jax.random.split(jax.random.key(seed), 8)
    return {
        "saved_inputs": bell_draw(key_list[0], (TOKENS, D), 1.0, 6.0, ((0, 32),)),
        "output_grads": bell_draw(key_list[1], (TOKENS, FF), 0.0625, 0.5, ((0, 32),)),
        "proj_in": bell_draw(key_list[2], (D, RANK_IN), D ** -0.5, 0.09375),
        "proj_out": bell_draw(key_list[3], (FF, RANK_OUT), FF ** -0.5, 0.046875),
        "doc_lengths": draw_doc_lengths(jax.random.fold_in(key_list[7], 71), 0),
        "device_docs": draw_device_docs(jax.random.fold_in(key_list[7], 71), 0),
        "fisher_inverse": draw_fisher_inverse(jax.random.fold_in(key_list[7], 71), 0),
    }


def reference(saved_inputs, output_grads, proj_in, proj_out, doc_lengths, device_docs, fisher_inverse):
    low_in = jnp.dot(saved_inputs, proj_in, preferred_element_type=jnp.float32).astype(jnp.bfloat16)
    low_out = jnp.dot(output_grads, proj_out, preferred_element_type=jnp.float32).astype(jnp.bfloat16)
    doc_ends = jnp.cumsum(doc_lengths)
    starts = doc_ends - doc_lengths
    positions = jnp.arange(TOKENS, dtype=jnp.int32)
    doc_ids = jnp.sum((starts[None, :] <= positions[:, None]).astype(jnp.int32), axis=1) - 1
    block_count = TOKENS // TOK_DEV
    ids_blocks = doc_ids.reshape(block_count, TOK_DEV)
    in_blocks = low_in.reshape(block_count, TOK_DEV, RANK_IN)
    out_blocks = low_out.reshape(block_count, TOK_DEV, RANK_OUT)
    doc_range = jnp.arange(NDOC, dtype=jnp.int32)

    def accumulate(total, pieces):
        block_ids, rows_in, rows_out = pieces
        onehot = (block_ids[:, None] == doc_range[None, :]).astype(rows_out.dtype)
        masked = (onehot[:, :, None] * rows_out[:, None, :]).reshape(TOK_DEV, NDOC * RANK_OUT)
        term = lax.dot_general(masked, rows_in, (((0,), (0,)), ((), ())), preferred_element_type=jnp.float32)
        return total + term, None

    start_total = jnp.zeros((NDOC * RANK_OUT, RANK_IN), jnp.float32)
    total, _ = lax.scan(accumulate, start_total, (ids_blocks, in_blocks, out_blocks))
    grads = total.reshape(NDOC, NFEAT)
    owned = grads[device_docs.astype(jnp.int32)]
    return jnp.dot(owned, fisher_inverse, precision=lax.Precision.HIGHEST, preferred_element_type=jnp.float32)
```

```python
import functools

import jax
import jax.numpy as jnp
from jax import lax
from jax.experimental import pallas as pl
from jax.experimental.pallas import tpu as pltpu
from jax.sharding import PartitionSpec as P

SLOTS = 5
STEPS = 8
MIB = 1024 * 1024


def doc_ends(lens):
    docs = lens.shape[1]
    row = lax.broadcasted_iota(jnp.int32, (docs, docs), 0)
    col = lax.broadcasted_iota(jnp.int32, (docs, docs), 1)
    wide = jnp.broadcast_to(lens.astype(jnp.float32), (docs, docs))
    return jnp.sum(jnp.where(col <= row, wide, 0.0), axis=1, keepdims=True)


def docs_at(ends, positions):
    return jnp.sum(jnp.where(ends <= positions, 1.0, 0.0), axis=0, keepdims=True)


def partials_kernel(n_col, lens, x_in, x_out, w_in, w_out, out, acc_in, acc_out):
    step = pl.program_id(0)

    @pl.when(step == 0)
    def _():
        acc_in[...] = jnp.zeros_like(acc_in)
        acc_out[...] = jnp.zeros_like(acc_out)

    acc_in[...] += jnp.dot(x_in[...], w_in[...], preferred_element_type=jnp.float32)
    acc_out[...] += jnp.dot(x_out[...], w_out[...], preferred_element_type=jnp.float32)

    @pl.when(step == pl.num_programs(0) - 1)
    def _():
        tokens = acc_out.shape[0]
        shard = lax.axis_index("row") * n_col + lax.axis_index("col")
        base = (shard * tokens).astype(jnp.float32)
        ends = doc_ends(lens[...])
        token = lax.broadcasted_iota(jnp.int32, (1, tokens), 1).astype(jnp.float32)
        slot = docs_at(ends, token + base) - docs_at(ends, jnp.zeros((1, tokens)) + base)
        low_in = acc_in[...].astype(jnp.bfloat16)
        low_out = acc_out[...].astype(jnp.bfloat16).astype(jnp.float32).T
        devices, _, rows, _ = out.shape
        for s in range(SLOTS):
            masked = jnp.where(slot == float(s), low_out, 0.0).astype(jnp.bfloat16)
            part = jnp.dot(masked, low_in, preferred_element_type=jnp.float32)
            for j in range(devices):
                out[j, s] = part[j * rows : (j + 1) * rows]


def partials_call(x_in, x_out, w_in, w_out, lens, n_col, devices):
    tokens, d_in = x_in.shape
    d_out, rank_out = w_out.shape
    rank_in = w_in.shape[1]
    k_in, k_out = d_in // STEPS, d_out // STEPS
    return pl.pallas_call(
        functools.partial(partials_kernel, n_col),
        grid=(STEPS,),
        in_specs=[
            pl.BlockSpec(lens.shape, lambda i: (0, 0)),
            pl.BlockSpec((tokens, k_in), lambda i: (0, i)),
            pl.BlockSpec((tokens, k_out), lambda i: (0, i)),
            pl.BlockSpec((k_in, rank_in), lambda i: (i, 0)),
            pl.BlockSpec((k_out, rank_out), lambda i: (i, 0)),
        ],
        out_specs=pl.BlockSpec(
            (devices, SLOTS, rank_out // devices, rank_in), lambda i: (0, 0, 0, 0)
        ),
        out_shape=jax.ShapeDtypeStruct(
            (devices, SLOTS, rank_out // devices, rank_in), jnp.float32
        ),
        scratch_shapes=[
            pltpu.VMEM((tokens, rank_in), jnp.float32),
            pltpu.VMEM((tokens, rank_out), jnp.float32),
        ],
        compiler_params=pltpu.CompilerParams(vmem_limit_bytes=16 * MIB),
        name="partials",
    )(lens, x_in, x_out, w_in, w_out)


def narrow_kernel(f_ref, out):
    out[...] = f_ref[...].astype(jnp.bfloat16)


def narrow_call(fisher):
    rows, cols = fisher.shape
    step = min(rows, 128)
    return pl.pallas_call(
        narrow_kernel,
        grid=(rows // step,),
        in_specs=[pl.BlockSpec((step, cols), lambda i: (i, 0))],
        out_specs=pl.BlockSpec((step, cols), lambda i: (i, 0)),
        out_shape=jax.ShapeDtypeStruct((rows, cols), jnp.bfloat16),
        compiler_params=pltpu.CompilerParams(vmem_limit_bytes=16 * MIB),
        cost_estimate=pl.CostEstimate(
            flops=rows * cols, bytes_accessed=6 * rows * cols, transcendentals=0
        ),
        name="narrow",
    )(fisher)


def combine_kernel(tokens, lens, docs_row, got, out):
    docs = lens.shape[1]
    pieces, rank = got.shape
    rows = out.shape[1] // rank
    slots = pieces // rows
    ends = doc_ends(lens[...])
    m = lax.broadcasted_iota(jnp.int32, (1, slots), 1)
    source = lax.shift_right_logical(m * 52429, 18)
    first = docs_at(ends, (source * tokens).astype(jnp.float32))
    doc = first + (m - source * SLOTS).astype(jnp.float32)
    row = lax.broadcasted_iota(jnp.int32, (docs, docs), 0)
    col = lax.broadcasted_iota(jnp.int32, (docs, docs), 1)
    wanted = jnp.broadcast_to(docs_row[...].astype(jnp.float32), (docs, docs))
    wanted = jnp.sum(jnp.where(col == row, wanted, 0.0), axis=1, keepdims=True)
    onehot = jnp.where(wanted == doc, 1.0, 0.0)
    for p in range(rows):
        piece = got[pl.ds(p, slots, stride=rows), :]
        out[:, p * rank : (p + 1) * rank] = jnp.dot(
            onehot, piece, precision=lax.Precision.HIGHEST, preferred_element_type=jnp.float32
        )


def combine_call(got, lens, docs_row, tokens):
    devices, slots, rows, rank = got.shape
    docs = lens.shape[1]
    return pl.pallas_call(
        functools.partial(combine_kernel, tokens),
        out_shape=jax.ShapeDtypeStruct((docs, rows * rank), jnp.float32),
        compiler_params=pltpu.CompilerParams(vmem_limit_bytes=16 * MIB),
        name="combine",
    )(lens, docs_row, got.reshape(devices * slots * rows, rank))


def product_kernel(n_parts, *refs):
    parts, (f_ref, out) = refs[:n_parts], refs[n_parts:]
    docs, size = parts[0].shape
    me = lax.axis_index("col")
    groups, rows, _ = out.shape
    highs, lows = [], []
    for part in parts:
        high = part[...].astype(jnp.bfloat16)
        highs.append(high)
        lows.append((part[...] - high.astype(jnp.float32)).astype(jnp.bfloat16))
    both = [jnp.concatenate([h, l], axis=0) for h, l in zip(highs, lows)]
    cols = f_ref.shape[1]
    width = 512 if cols % 512 == 0 else cols
    for n in range(cols // width):
        total = jnp.zeros((2 * docs, width), jnp.float32)
        for k in range(n_parts):
            at = pl.multiple_of(jnp.bitwise_xor(me, k) * size, size)
            tile = f_ref[pl.ds(at, size), n * width : (n + 1) * width]
            total += jnp.dot(both[k], tile, preferred_element_type=jnp.float32)
        total = total[:docs] + total[docs:]
        for g in range(groups):
            out[g, :, n * width : (n + 1) * width] = total[g * rows : (g + 1) * rows]


def product_call(parts, fisher, groups):
    docs = parts[0].shape[0]
    cols = fisher.shape[1]
    n = len(parts)
    return pl.pallas_call(
        functools.partial(product_kernel, n),
        out_shape=jax.ShapeDtypeStruct((groups, docs // groups, cols), jnp.float32),
        compiler_params=pltpu.CompilerParams(vmem_limit_bytes=40 * MIB),
        name="product",
    )(*parts, fisher)


def exchange(x, axis, bit):
    size = lax.axis_size(axis)
    return lax.ppermute(x, axis, [(i, i ^ bit) for i in range(size)])


def per_device(
    saved_inputs, output_grads, proj_in, proj_out, doc_lengths, device_docs, fisher_inverse
):
    tokens = saved_inputs.shape[0]
    n_row, n_col = lax.axis_size("row"), lax.axis_size("col")
    devices = n_row * n_col
    lens = doc_lengths.reshape(1, -1)
    docs_row = device_docs.reshape(1, -1)
    partials = partials_call(
        saved_inputs, output_grads, proj_in, proj_out, lens, n_col, devices
    )
    got = lax.all_to_all(partials, ("row", "col"), 0, 0, tiled=True)
    fisher = narrow_call(fisher_inverse)
    mine = combine_call(got, lens, docs_row, tokens)
    parts = {0: mine}
    bit = n_col // 2
    while bit:
        parts.update({k ^ bit: exchange(v, "col", bit) for k, v in list(parts.items())})
        bit //= 2
    sums = product_call([parts[k] for k in range(n_col)], fisher, n_row)
    shares = lax.all_to_all(sums, "row", 0, 0, tiled=True)
    return jnp.sum(shares, axis=0)


def solution(mesh):
    placed = (P(("row", "col"), None), P(("row", "col"), None), P(), P(), P(), P(), P("row", "col"))
    return jax.shard_map(
        per_device, mesh=mesh, in_specs=placed, out_specs=P("row", "col"), check_vma=False
    )
```

```python
import functools

import jax
import jax.numpy as jnp
from jax import lax
from jax.experimental import pallas as pl
from jax.experimental.pallas import tpu as pltpu
from jax.sharding import PartitionSpec as P


SLOTS = 5
STEPS = 8
MIB = 1024 * 1024


def doc_ends(lens):
    docs = lens.shape[1]
    row = lax.broadcasted_iota(jnp.int32, (docs, docs), 0)
    col = lax.broadcasted_iota(jnp.int32, (docs, docs), 1)
    wide = jnp.broadcast_to(lens.astype(jnp.float32), (docs, docs))
    return jnp.sum(jnp.where(col <= row, wide, 0.0), axis=1, keepdims=True)


def docs_at(ends, positions):
    return jnp.sum(jnp.where(ends <= positions, 1.0, 0.0), axis=0, keepdims=True)


def partials_kernel(n_col, lens, x_in, x_out, w_in, w_out, out, acc_in, acc_out):
    step = pl.program_id(0)

    @pl.when(step == 0)
    def _():
        acc_in[...] = jnp.zeros_like(acc_in)
        acc_out[...] = jnp.zeros_like(acc_out)

    acc_in[...] += jnp.dot(x_in[...], w_in[...], preferred_element_type=jnp.float32)
    acc_out[...] += jnp.dot(x_out[...], w_out[...], preferred_element_type=jnp.float32)

    @pl.when(step == pl.num_programs(0) - 1)
    def _():
        tokens = acc_out.shape[0]
        shard = lax.axis_index("row") * n_col + lax.axis_index("col")
        base = (shard * tokens).astype(jnp.float32)
        ends = doc_ends(lens[...])
        token = lax.broadcasted_iota(jnp.int32, (1, tokens), 1).astype(jnp.float32)
        slot = docs_at(ends, token + base) - docs_at(ends, jnp.zeros((1, tokens)) + base)
        low_in = acc_in[...].astype(jnp.bfloat16)
        low_out = acc_out[...].astype(jnp.bfloat16).astype(jnp.float32).T
        devices, _, rows, _ = out.shape
        for s in range(SLOTS):
            masked = jnp.where(slot == float(s), low_out, 0.0).astype(jnp.bfloat16)
            part = jnp.dot(masked, low_in, preferred_element_type=jnp.float32)
            for j in range(devices):
                out[j, s] = part[j * rows : (j + 1) * rows]


def partials_call(x_in, x_out, w_in, w_out, lens, n_col, devices):
    tokens, d_in = x_in.shape
    d_out, rank_out = w_out.shape
    rank_in = w_in.shape[1]
    k_in, k_out = d_in // STEPS, d_out // STEPS
    return pl.pallas_call(
        functools.partial(partials_kernel, n_col),
        grid=(STEPS,),
        in_specs=[
            pl.BlockSpec(lens.shape, lambda i: (0, 0)),
            pl.BlockSpec((tokens, k_in), lambda i: (0, i)),
            pl.BlockSpec((tokens, k_out), lambda i: (0, i)),
            pl.BlockSpec((k_in, rank_in), lambda i: (i, 0)),
            pl.BlockSpec((k_out, rank_out), lambda i: (i, 0)),
        ],
        out_specs=pl.BlockSpec(
            (devices, SLOTS, rank_out // devices, rank_in), lambda i: (0, 0, 0, 0)
        ),
        out_shape=jax.ShapeDtypeStruct(
            (devices, SLOTS, rank_out // devices, rank_in), jnp.float32
        ),
        scratch_shapes=[
            pltpu.VMEM((tokens, rank_in), jnp.float32),
            pltpu.VMEM((tokens, rank_out), jnp.float32),
        ],
        compiler_params=pltpu.CompilerParams(vmem_limit_bytes=60 * MIB),
        name="partials",
    )(lens, x_in, x_out, w_in, w_out)


def narrow_kernel(me, f_ref, out):
    del me
    out[...] = f_ref[...].astype(jnp.bfloat16)


def narrow_call(me, fisher, n_parts):
    rows, cols = fisher.shape
    size = rows // n_parts
    step = min(size, 256)
    count = size // step
    return pl.pallas_call(
        narrow_kernel,
        grid_spec=pltpu.PrefetchScalarGridSpec(
            num_scalar_prefetch=1,
            grid=(n_parts - 1, count),
            in_specs=[
                pl.BlockSpec(
                    (step, cols),
                    lambda k, i, me: (jnp.bitwise_xor(me[0], k + 1) * count + i, 0),
                )
            ],
            out_specs=pl.BlockSpec((step, cols), lambda k, i, me: (k * count + i, 0)),
        ),
        out_shape=jax.ShapeDtypeStruct((rows - size, cols), jnp.bfloat16),
        compiler_params=pltpu.CompilerParams(vmem_limit_bytes=60 * MIB),
        cost_estimate=pl.CostEstimate(
            flops=rows * cols, bytes_accessed=6 * (rows - size) * cols, transcendentals=0
        ),
        name="narrow",
    )(me, fisher)


def combine_kernel(tokens, lens, docs_row, got, out):
    docs = lens.shape[1]
    pieces, rank = got.shape
    rows = out.shape[1] // rank
    slots = pieces // rows
    ends = doc_ends(lens[...])
    m = lax.broadcasted_iota(jnp.int32, (1, slots), 1)
    source = lax.shift_right_logical(m * 52429, 18)
    first = docs_at(ends, (source * tokens).astype(jnp.float32))
    doc = first + (m - source * SLOTS).astype(jnp.float32)
    row = lax.broadcasted_iota(jnp.int32, (docs, docs), 0)
    col = lax.broadcasted_iota(jnp.int32, (docs, docs), 1)
    wanted = jnp.broadcast_to(docs_row[...].astype(jnp.float32), (docs, docs))
    wanted = jnp.sum(jnp.where(col == row, wanted, 0.0), axis=1, keepdims=True)
    onehot = jnp.where(wanted == doc, 1.0, 0.0)
    for p in range(rows):
        piece = got[pl.ds(p, slots, stride=rows), :]
        out[:, p * rank : (p + 1) * rank] = jnp.dot(
            onehot, piece, precision=lax.Precision.HIGHEST, preferred_element_type=jnp.float32
        )


def combine_call(got, lens, docs_row, tokens):
    devices, slots, rows, rank = got.shape
    docs = lens.shape[1]
    return pl.pallas_call(
        functools.partial(combine_kernel, tokens),
        out_shape=jax.ShapeDtypeStruct((docs, rows * rank), jnp.float32),
        compiler_params=pltpu.CompilerParams(vmem_limit_bytes=16 * MIB),
        name="combine",
    )(lens, docs_row, got.reshape(devices * slots * rows, rank))


def split(x):
    high = x.astype(jnp.bfloat16)
    low = (x - high.astype(jnp.float32)).astype(jnp.bfloat16)
    return jnp.concatenate([high, low], axis=0)


def own_kernel(me, part, f_ref, out):
    del me
    docs = part.shape[0]
    total = jnp.dot(
        split(part[...]), f_ref[...].astype(jnp.bfloat16), preferred_element_type=jnp.float32
    )
    out[...] = total[:docs] + total[docs:]


def own_call(me, part, fisher):
    docs, size = part.shape
    cols = fisher.shape[1]
    width = 1024 if cols % 1024 == 0 else cols
    return pl.pallas_call(
        own_kernel,
        grid_spec=pltpu.PrefetchScalarGridSpec(
            num_scalar_prefetch=1,
            grid=(cols // width,),
            in_specs=[
                pl.BlockSpec((docs, size), lambda n, me: (0, 0)),
                pl.BlockSpec((size, width), lambda n, me: (me[0], n)),
            ],
            out_specs=pl.BlockSpec((docs, width), lambda n, me: (0, n)),
        ),
        out_shape=jax.ShapeDtypeStruct((docs, cols), jnp.float32),
        compiler_params=pltpu.CompilerParams(vmem_limit_bytes=40 * MIB),
        cost_estimate=pl.CostEstimate(
            flops=4 * docs * size * cols, bytes_accessed=4 * size * cols, transcendentals=0
        ),
        name="own",
    )(me, part, fisher)


def product_kernel(n_parts, *refs):
    parts, (f_ref, first, out) = refs[:n_parts], refs[n_parts:]
    docs, size = parts[0].shape
    groups, rows, _ = out.shape
    total = jnp.zeros((2 * docs, f_ref.shape[1]), jnp.float32)
    for k, part in enumerate(parts):
        total += jnp.dot(
            split(part[...]),
            f_ref[k * size : (k + 1) * size, :],
            preferred_element_type=jnp.float32,
        )
    total = first[...] + (total[:docs] + total[docs:])
    for g in range(groups):
        out[g] = total[g * rows : (g + 1) * rows]


def product_call(parts, fisher, first, groups):
    docs, size = parts[0].shape
    n = len(parts)
    rows, cols = fisher.shape
    width = 512 if cols % 512 == 0 else cols
    return pl.pallas_call(
        functools.partial(product_kernel, n),
        grid=(cols // width,),
        in_specs=[pl.BlockSpec((docs, size), lambda i: (0, 0))] * n
        + [
            pl.BlockSpec((rows, width), lambda i: (0, i)),
            pl.BlockSpec((docs, width), lambda i: (0, i)),
        ],
        out_specs=pl.BlockSpec((groups, docs // groups, width), lambda i: (0, 0, i)),
        out_shape=jax.ShapeDtypeStruct((groups, docs // groups, cols), jnp.float32),
        compiler_params=pltpu.CompilerParams(vmem_limit_bytes=32 * MIB),
        name="product",
    )(*parts, fisher, first)


def exchange(x, axis, bit):
    size = lax.axis_size(axis)
    return lax.ppermute(x, axis, [(i, i ^ bit) for i in range(size)])


def per_device(
    saved_inputs, output_grads, proj_in, proj_out, doc_lengths, device_docs, fisher_inverse
):
    tokens = saved_inputs.shape[0]
    n_row, n_col = lax.axis_size("row"), lax.axis_size("col")
    devices = n_row * n_col
    lens = doc_lengths.reshape(1, -1)
    docs_row = device_docs.reshape(1, -1)
    me = lax.axis_index("col").astype(jnp.int32).reshape(1)
    partials = partials_call(
        saved_inputs, output_grads, proj_in, proj_out, lens, n_col, devices
    )
    got = lax.all_to_all(partials, ("row", "col"), 0, 0, tiled=True)
    others = narrow_call(me, fisher_inverse, n_col)
    mine = combine_call(got, lens, docs_row, tokens)
    parts = {0: mine}
    bit = n_col // 2
    while bit:
        held = dict(parts)
        for k, v in held.items():
            parts[k ^ bit] = exchange(v, "col", bit)
        bit //= 2
    first = own_call(me, mine, fisher_inverse)
    sums = product_call([parts[k] for k in range(1, n_col)], others, first, n_row)
    shares = lax.all_to_all(sums, "row", 0, 0, tiled=True)
    return jnp.sum(shares, axis=0)


def solution(mesh):
    placed = (P(("row", "col"), None), P(("row", "col"), None), P(), P(), P(), P(), P("row", "col"))
    return jax.shard_map(
        per_device, mesh=mesh, in_specs=placed, out_specs=P("row", "col"), check_vma=False
    )
```

```python
import functools

import jax
import jax.numpy as jnp
from jax import lax
from jax.experimental import pallas as pl
from jax.experimental.pallas import tpu as pltpu
from jax.sharding import PartitionSpec as P


SLOTS = 5
STEPS = 8
MIB = 1024 * 1024


def doc_ends(lens):
    docs = lens.shape[1]
    row = lax.broadcasted_iota(jnp.int32, (docs, docs), 0)
    col = lax.broadcasted_iota(jnp.int32, (docs, docs), 1)
    wide = jnp.broadcast_to(lens.astype(jnp.float32), (docs, docs))
    return jnp.sum(jnp.where(col <= row, wide, 0.0), axis=1, keepdims=True)


def docs_at(ends, positions):
    return jnp.sum(jnp.where(ends <= positions, 1.0, 0.0), axis=0, keepdims=True)


def partials_kernel(n_col, lens, x_in, x_out, w_in, w_out, out, b_in, b_out, v_in, v_out, sems):
    tokens, rank_out = b_out.shape[0], w_out.shape[1]
    k_in, k_out = x_in.shape[1] // STEPS, x_out.shape[1] // STEPS
    copies = []
    for i in range(STEPS):
        at_in, at_out = pl.ds(i * k_in, k_in), pl.ds(i * k_out, k_out)
        copies.append(
            [
                pltpu.make_async_copy(x_out.at[:, at_out], b_out.at[:, at_out], sems.at[0, i]),
                pltpu.make_async_copy(w_out.at[at_out, :], v_out.at[at_out, :], sems.at[1, i]),
                pltpu.make_async_copy(x_in.at[:, at_in], b_in.at[:, at_in], sems.at[2, i]),
                pltpu.make_async_copy(w_in.at[at_in, :], v_in.at[at_in, :], sems.at[3, i]),
            ]
        )
    for group in copies:
        for copy in group:
            copy.start()
    shard = lax.axis_index("row") * n_col + lax.axis_index("col")
    base = (shard * tokens).astype(jnp.float32)
    ends = doc_ends(lens[...])
    token = lax.broadcasted_iota(jnp.int32, (1, tokens), 1).astype(jnp.float32)
    slot = docs_at(ends, token + base) - docs_at(ends, jnp.zeros((1, tokens)) + base)
    acc_in = jnp.zeros((tokens, w_in.shape[1]), jnp.float32)
    acc_out = jnp.zeros((tokens, rank_out), jnp.float32)
    for i in range(STEPS):
        at_in, at_out = pl.ds(i * k_in, k_in), pl.ds(i * k_out, k_out)
        for copy in copies[i]:
            copy.wait()
        acc_out += jnp.dot(
            b_out[:, at_out], v_out[at_out, :], preferred_element_type=jnp.float32
        )
        acc_in += jnp.dot(b_in[:, at_in], v_in[at_in, :], preferred_element_type=jnp.float32)
    low_in = acc_in.astype(jnp.bfloat16)
    low_out = acc_out.astype(jnp.bfloat16).astype(jnp.float32).T
    devices, _, rows, _ = out.shape
    for s in range(SLOTS):
        masked = jnp.where(slot == float(s), low_out, 0.0).astype(jnp.bfloat16)
        part = jnp.dot(masked, low_in, preferred_element_type=jnp.float32)
        for j in range(devices):
            out[j, s] = part[j * rows : (j + 1) * rows]


def partials_call(x_in, x_out, w_in, w_out, lens, n_col, devices):
    rank_in, rank_out = w_in.shape[1], w_out.shape[1]
    far = pl.BlockSpec(memory_space=pltpu.HBM)
    return pl.pallas_call(
        functools.partial(partials_kernel, n_col),
        in_specs=[pl.BlockSpec(memory_space=pltpu.VMEM), far, far, far, far],
        out_specs=pl.BlockSpec(memory_space=pltpu.VMEM),
        out_shape=pltpu.VMEM((devices, SLOTS, rank_out // devices, rank_in), jnp.float32),
        scratch_shapes=[
            pltpu.VMEM(x_in.shape, x_in.dtype),
            pltpu.VMEM(x_out.shape, x_out.dtype),
            pltpu.VMEM(w_in.shape, w_in.dtype),
            pltpu.VMEM(w_out.shape, w_out.dtype),
            pltpu.SemaphoreType.DMA((4, STEPS)),
        ],
        compiler_params=pltpu.CompilerParams(vmem_limit_bytes=62_495_744),
        name="partials",
    )(lens, x_in, x_out, w_in, w_out)


def pause_kernel(out):
    del out


def pause_call():
    return pl.pallas_call(
        pause_kernel,
        out_specs=pl.BlockSpec(memory_space=pltpu.SMEM),
        out_shape=jax.ShapeDtypeStruct((1,), jnp.int32),
        compiler_params=pltpu.CompilerParams(vmem_limit_bytes=MIB, has_side_effects=True),
        cost_estimate=pl.CostEstimate(
            flops=10_000_000_000, bytes_accessed=30_000_000, transcendentals=0
        ),
        name="pause",
    )()


def combine_kernel(tokens, lens, docs_row, got, out):
    docs = lens.shape[1]
    pieces, rank = got.shape
    rows = out.shape[1] // rank
    slots = pieces // rows
    ends = doc_ends(lens[...])
    m = lax.broadcasted_iota(jnp.int32, (1, slots), 1)
    source = lax.shift_right_logical(m * 52429, 18)
    first = docs_at(ends, (source * tokens).astype(jnp.float32))
    doc = first + (m - source * SLOTS).astype(jnp.float32)
    row = lax.broadcasted_iota(jnp.int32, (docs, docs), 0)
    col = lax.broadcasted_iota(jnp.int32, (docs, docs), 1)
    wanted = jnp.broadcast_to(docs_row[...].astype(jnp.float32), (docs, docs))
    wanted = jnp.sum(jnp.where(col == row, wanted, 0.0), axis=1, keepdims=True)
    onehot = jnp.where(wanted == doc, 1.0, 0.0)
    for p in range(rows):
        piece = got[pl.ds(p, slots, stride=rows), :]
        out[:, p * rank : (p + 1) * rank] = jnp.dot(
            onehot, piece, precision=lax.Precision.HIGHEST, preferred_element_type=jnp.float32
        )


def combine_call(got, lens, docs_row, tokens):
    devices, slots, rows, rank = got.shape
    docs = lens.shape[1]
    return pl.pallas_call(
        functools.partial(combine_kernel, tokens),
        out_shape=jax.ShapeDtypeStruct((docs, rows * rank), jnp.float32),
        compiler_params=pltpu.CompilerParams(vmem_limit_bytes=4 * MIB),
        name="combine",
    )(lens, docs_row, got.reshape(devices * slots * rows, rank))


def split(x):
    high = x.astype(jnp.bfloat16)
    low = (x - high.astype(jnp.float32)).astype(jnp.bfloat16)
    return jnp.concatenate([high, low], axis=0)


def product_kernel(at, has_first, *refs):
    parts, refs = refs[: len(at)], refs[len(at) :]
    f_ref, out = refs[0], refs[-1]
    docs, size = parts[0].shape
    cols = f_ref.shape[1]
    me = lax.axis_index("col")
    both = [split(part[...]) for part in parts]
    width = 512 if cols % 512 == 0 else cols
    for n in range(cols // width):
        where = slice(n * width, (n + 1) * width)
        total = jnp.zeros((2 * docs, width), jnp.float32)
        for k, x in zip(at, both):
            rows = pl.ds(pl.multiple_of(jnp.bitwise_xor(me, k) * size, size), size)
            tile = f_ref[rows, where].astype(jnp.bfloat16)
            total += jnp.dot(x, tile, preferred_element_type=jnp.float32)
        total = total[:docs] + total[docs:]
        if has_first:
            total += refs[1][:, where]
        if out.ndim == 2:
            out[:, where] = total
        else:
            groups, height, _ = out.shape
            for g in range(groups):
                out[g, :, where] = total[g * height : (g + 1) * height]


def product_call(parts, at, fisher, first, groups):
    docs = parts[at[0]].shape[0]
    cols = fisher.shape[1]
    shape = (docs, cols) if groups is None else (groups, docs // groups, cols)
    args = [parts[k] for k in at] + [fisher] + ([] if first is None else [first])
    return pl.pallas_call(
        functools.partial(product_kernel, at, first is not None),
        in_specs=[pl.BlockSpec(memory_space=pltpu.VMEM)] * len(args),
        out_specs=pl.BlockSpec(memory_space=pltpu.VMEM),
        out_shape=jax.ShapeDtypeStruct(shape, jnp.float32),
        compiler_params=pltpu.CompilerParams(vmem_limit_bytes=12 * MIB),
    )(*args)


def exchange(x, axis, bit):
    size = lax.axis_size(axis)
    return lax.ppermute(x, axis, [(i, i ^ bit) for i in range(size)])


def per_device(
    saved_inputs, output_grads, proj_in, proj_out, doc_lengths, device_docs, fisher_inverse
):
    tokens = saved_inputs.shape[0]
    n_row, n_col = lax.axis_size("row"), lax.axis_size("col")
    devices = n_row * n_col
    lens = doc_lengths.reshape(1, -1)
    docs_row = device_docs.reshape(1, -1)
    fisher = pltpu.with_memory_space_constraint(fisher_inverse, pltpu.VMEM)
    partials = partials_call(saved_inputs, output_grads, proj_in, proj_out, lens, n_col, devices)
    pause_call()
    got = lax.all_to_all(partials, ("row", "col"), 0, 0, tiled=True)
    mine = combine_call(got, lens, docs_row, tokens)
    parts = {0: mine}
    bit = n_col // 2
    parts[bit] = exchange(mine, "col", bit)
    parts[1] = exchange(mine, "col", 1)
    while bit > 2:
        bit //= 2
        for k in [k for k in parts if k != 1]:
            parts[k ^ bit] = exchange(parts[k], "col", bit)
    evens = [k for k in parts if k > 1]
    for k in evens:
        parts[k ^ 1] = exchange(parts[k], "col", 1)
    sums = product_call(parts, list(range(n_col)), fisher, None, n_row)
    shares = lax.all_to_all(sums, "row", 0, 0, tiled=True)
    return jnp.sum(shares, axis=0)


def solution(mesh):
    placed = (P(("row", "col"), None), P(("row", "col"), None), P(), P(), P(), P(), P("row", "col"))
    return jax.shard_map(
        per_device, mesh=mesh, in_specs=placed, out_specs=P("row", "col"), check_vma=False
    )
```

```python
import functools

import jax
import jax.numpy as jnp
from jax import lax
from jax.experimental import pallas as pl
from jax.experimental.pallas import tpu as pltpu
from jax.sharding import PartitionSpec as P


SLOTS = 5
STEPS = 8
MIB = 1024 * 1024


def doc_ends(lens):
    docs = lens.shape[1]
    row = lax.broadcasted_iota(jnp.int32, (docs, docs), 0)
    col = lax.broadcasted_iota(jnp.int32, (docs, docs), 1)
    wide = jnp.broadcast_to(lens.astype(jnp.float32), (docs, docs))
    return jnp.sum(jnp.where(col <= row, wide, 0.0), axis=1, keepdims=True)


def docs_at(ends, positions):
    return jnp.sum(jnp.where(ends <= positions, 1.0, 0.0), axis=0, keepdims=True)


def partials_kernel(
    n_col, lens, x_in, x_out, w_in, w_out, tile, out, b_in, b_out, v_in, v_out, sems
):
    del tile
    tokens, rank_out = b_out.shape[0], w_out.shape[1]
    k_in, k_out = x_in.shape[1] // STEPS, x_out.shape[1] // STEPS
    copies = []
    for i in range(STEPS):
        at_in, at_out = pl.ds(i * k_in, k_in), pl.ds(i * k_out, k_out)
        copies.append(
            [
                pltpu.make_async_copy(x_out.at[:, at_out], b_out.at[:, at_out], sems.at[0, i]),
                pltpu.make_async_copy(w_out.at[at_out, :], v_out.at[at_out, :], sems.at[1, i]),
                pltpu.make_async_copy(x_in.at[:, at_in], b_in.at[:, at_in], sems.at[2, i]),
                pltpu.make_async_copy(w_in.at[at_in, :], v_in.at[at_in, :], sems.at[3, i]),
            ]
        )
    for group in copies:
        for copy in group:
            copy.start()
    shard = lax.axis_index("row") * n_col + lax.axis_index("col")
    base = (shard * tokens).astype(jnp.float32)
    ends = doc_ends(lens[...])
    token = lax.broadcasted_iota(jnp.int32, (1, tokens), 1).astype(jnp.float32)
    slot = docs_at(ends, token + base) - docs_at(ends, jnp.zeros((1, tokens)) + base)
    acc_in = jnp.zeros((tokens, w_in.shape[1]), jnp.float32)
    acc_out = jnp.zeros((tokens, rank_out), jnp.float32)
    for i in range(STEPS):
        at_in, at_out = pl.ds(i * k_in, k_in), pl.ds(i * k_out, k_out)
        for copy in copies[i]:
            copy.wait()
        acc_out += jnp.dot(
            b_out[:, at_out], v_out[at_out, :], preferred_element_type=jnp.float32
        )
        acc_in += jnp.dot(b_in[:, at_in], v_in[at_in, :], preferred_element_type=jnp.float32)
    low_in = acc_in.astype(jnp.bfloat16)
    low_out = acc_out.astype(jnp.bfloat16).astype(jnp.float32).T
    devices, _, rows, _ = out.shape
    for s in range(SLOTS):
        masked = jnp.where(slot == float(s), low_out, 0.0).astype(jnp.bfloat16)
        part = jnp.dot(masked, low_in, preferred_element_type=jnp.float32)
        for j in range(devices):
            out[j, s] = part[j * rows : (j + 1) * rows]


def partials_call(x_in, x_out, w_in, w_out, lens, tile, n_col, devices):
    rank_in, rank_out = w_in.shape[1], w_out.shape[1]
    far = pl.BlockSpec(memory_space=pltpu.HBM)
    return pl.pallas_call(
        functools.partial(partials_kernel, n_col),
        in_specs=[pl.BlockSpec(memory_space=pltpu.VMEM)] + [far] * 5,
        out_specs=pl.BlockSpec(memory_space=pltpu.VMEM),
        out_shape=pltpu.VMEM((devices, SLOTS, rank_out // devices, rank_in), jnp.float32),
        scratch_shapes=[
            pltpu.VMEM(x_in.shape, x_in.dtype),
            pltpu.VMEM(x_out.shape, x_out.dtype),
            pltpu.VMEM(w_in.shape, w_in.dtype),
            pltpu.VMEM(w_out.shape, w_out.dtype),
            pltpu.SemaphoreType.DMA((4, STEPS)),
        ],
        compiler_params=pltpu.CompilerParams(vmem_limit_bytes=62_495_744),
        name="partials",
    )(lens, x_in, x_out, w_in, w_out, pltpu.with_memory_space_constraint(tile, pltpu.HBM))


def pause_kernel(*refs):
    del refs


def pause_call(*after):
    return pl.pallas_call(
        pause_kernel,
        in_specs=[pl.BlockSpec(memory_space=pltpu.VMEM)] * len(after),
        out_specs=pl.BlockSpec(memory_space=pltpu.VMEM),
        out_shape=pltpu.VMEM((8, 128), jnp.float32),
        compiler_params=pltpu.CompilerParams(vmem_limit_bytes=MIB, has_side_effects=True),
        cost_estimate=pl.CostEstimate(
            flops=12_000_000_000, bytes_accessed=36_000_000, transcendentals=0
        ),
        name="pause",
    )(*after)


def combine_kernel(tokens, lens, docs_row, got, out):
    docs = lens.shape[1]
    pieces, rank = got.shape
    rows = out.shape[1] // rank
    slots = pieces // rows
    ends = doc_ends(lens[...])
    m = lax.broadcasted_iota(jnp.int32, (1, slots), 1)
    source = lax.shift_right_logical(m * 52429, 18)
    first = docs_at(ends, (source * tokens).astype(jnp.float32))
    doc = first + (m - source * SLOTS).astype(jnp.float32)
    row = lax.broadcasted_iota(jnp.int32, (docs, docs), 0)
    col = lax.broadcasted_iota(jnp.int32, (docs, docs), 1)
    wanted = jnp.broadcast_to(docs_row[...].astype(jnp.float32), (docs, docs))
    wanted = jnp.sum(jnp.where(col == row, wanted, 0.0), axis=1, keepdims=True)
    onehot = jnp.where(wanted == doc, 1.0, 0.0)
    for p in range(rows):
        piece = got[pl.ds(p, slots, stride=rows), :]
        out[:, p * rank : (p + 1) * rank] = jnp.dot(
            onehot, piece, precision=lax.Precision.HIGHEST, preferred_element_type=jnp.float32
        )


def combine_call(got, lens, docs_row, tokens):
    devices, slots, rows, rank = got.shape
    docs = lens.shape[1]
    return pl.pallas_call(
        functools.partial(combine_kernel, tokens),
        out_shape=jax.ShapeDtypeStruct((docs, rows * rank), jnp.float32),
        compiler_params=pltpu.CompilerParams(vmem_limit_bytes=4 * MIB),
        name="combine",
    )(lens, docs_row, got.reshape(devices * slots * rows, rank))


def split(x):
    high = x.astype(jnp.bfloat16)
    low = (x - high.astype(jnp.float32)).astype(jnp.bfloat16)
    return jnp.concatenate([high, low], axis=0)


def product_kernel(at, has_first, *refs):
    parts, refs = refs[: len(at)], refs[len(at) :]
    f_ref, outs = refs[0], refs[1 + has_first :]
    docs, size = parts[0].shape
    cols = f_ref.shape[1]
    me = lax.axis_index("col")
    both = [split(part[...]) for part in parts]
    width = 512 if cols % 512 == 0 else cols
    for n in range(cols // width):
        where = slice(n * width, (n + 1) * width)
        total = jnp.zeros((2 * docs, width), jnp.float32)
        for k, x in zip(at, both):
            rows = pl.ds(pl.multiple_of(jnp.bitwise_xor(me, k) * size, size), size)
            tile = f_ref[rows, where].astype(jnp.bfloat16)
            total += jnp.dot(x, tile, preferred_element_type=jnp.float32)
        total = total[:docs] + total[docs:]
        if has_first:
            total += refs[1][:, where]
        if len(outs) == 1:
            outs[0][:, where] = total
            continue
        groups, height, _ = outs[0].shape
        second = lax.rem(lax.axis_index("row"), 2) == 1
        for g in range(groups):
            a = total[2 * g * height : (2 * g + 1) * height]
            b = total[(2 * g + 1) * height : (2 * g + 2) * height]
            outs[0][g, :, where] = jnp.where(second, b, a)
            outs[1][g, :, where] = jnp.where(second, a, b)


def product_call(parts, at, fisher, first, groups):
    docs = parts[at[0]].shape[0]
    cols = fisher.shape[1]
    shape, count = (docs, cols), 1
    if groups is not None:
        shape, count = (groups // 2, docs // groups, cols), 2
    args = [parts[k] for k in at] + [fisher] + ([] if first is None else [first])
    return pl.pallas_call(
        functools.partial(product_kernel, at, first is not None),
        in_specs=[pl.BlockSpec(memory_space=pltpu.VMEM)] * len(args),
        out_specs=[pl.BlockSpec(memory_space=pltpu.VMEM)] * count,
        out_shape=[jax.ShapeDtypeStruct(shape, jnp.float32)] * count,
        compiler_params=pltpu.CompilerParams(vmem_limit_bytes=12 * MIB),
    )(*args)


def fold_kernel(mine, got, *outs):
    me = lax.div(lax.axis_index("row"), 2)
    for k, out in enumerate(outs):
        at = jnp.bitwise_xor(me, k)
        out[...] = mine[at] + got[at]


def fold_call(mine, got):
    pairs, height, cols = mine.shape
    return pl.pallas_call(
        fold_kernel,
        in_specs=[pl.BlockSpec(memory_space=pltpu.VMEM)] * 2,
        out_specs=[pl.BlockSpec(memory_space=pltpu.VMEM)] * pairs,
        out_shape=[jax.ShapeDtypeStruct((height, cols), jnp.float32)] * pairs,
        compiler_params=pltpu.CompilerParams(vmem_limit_bytes=4 * MIB),
        name="fold",
    )(mine, got)


def exchange(x, axis, bit):
    size = lax.axis_size(axis)
    return lax.ppermute(x, axis, [(i, i ^ bit) for i in range(size)])


def per_device(
    saved_inputs, output_grads, proj_in, proj_out, doc_lengths, device_docs, fisher_inverse
):
    tokens = saved_inputs.shape[0]
    n_row, n_col = lax.axis_size("row"), lax.axis_size("col")
    devices = n_row * n_col
    lens = doc_lengths.reshape(1, -1)
    docs_row = device_docs.reshape(1, -1)
    fisher = pltpu.with_memory_space_constraint(fisher_inverse, pltpu.VMEM)
    partials = partials_call(
        saved_inputs, output_grads, proj_in, proj_out, lens, fisher_inverse, n_col, devices
    )
    pause_call(pause_call())
    got = lax.all_to_all(partials, ("row", "col"), 0, 0, tiled=True)
    mine = combine_call(got, lens, docs_row, tokens)
    parts = {0: mine}
    bit = n_col // 2
    parts[bit] = exchange(mine, "col", bit)
    parts[1] = exchange(mine, "col", 1)
    while bit > 2:
        bit //= 2
        for k in [k for k in parts if k != 1]:
            parts[k ^ bit] = exchange(parts[k], "col", bit)
    evens = [k for k in parts if k > 1]
    for k in evens:
        parts[k ^ 1] = exchange(parts[k], "col", 1)
    (sums,) = product_call(parts, [0, 1], fisher, None, None)
    (sums,) = product_call(parts, evens, fisher, sums, None)
    odds = [k ^ 1 for k in evens]
    kept, given = product_call(parts, odds, fisher, sums, n_row)
    got = exchange(given, "row", 1)
    shares = list(fold_call(kept, got))
    total = shares[0]
    for k in range(len(shares) - 1, 0, -1):
        shares[k] = exchange(shares[k], "row", 2 * k)
    for k in range(1, len(shares)):
        total += shares[k]
    return total


def solution(mesh):
    placed = (P(("row", "col"), None), P(("row", "col"), None), P(), P(), P(), P(), P("row", "col"))
    return jax.shard_map(
        per_device, mesh=mesh, in_specs=placed, out_specs=P("row", "col"), check_vma=False
    )
```

```python
import functools

import jax
import jax.numpy as jnp
from jax import lax
from jax.experimental import pallas as pl
from jax.experimental.pallas import tpu as pltpu
from jax.sharding import PartitionSpec as P


SLOTS = 5
STEPS = 8
HALVES = 2
MIB = 1024 * 1024


def doc_ends(lens):
    docs = lens.shape[1]
    row = lax.broadcasted_iota(jnp.int32, (docs, docs), 0)
    col = lax.broadcasted_iota(jnp.int32, (docs, docs), 1)
    wide = jnp.broadcast_to(lens.astype(jnp.float32), (docs, docs))
    return jnp.sum(jnp.where(col <= row, wide, 0.0), axis=1, keepdims=True)


def docs_at(ends, positions):
    return jnp.sum(jnp.where(ends <= positions, 1.0, 0.0), axis=0, keepdims=True)


def partials_kernel(
    n_col, lens, x_in, x_out, w_in, w_out, tile, out, b_in, b_out, v_in, v_out, sems
):
    del tile
    tokens, rank_out = b_out.shape[0], w_out.shape[1]
    k_in, k_out = x_in.shape[1] // STEPS, x_out.shape[1] // STEPS
    copies = []
    for i in range(STEPS):
        at_in, at_out = pl.ds(i * k_in, k_in), pl.ds(i * k_out, k_out)
        copies.append(
            [
                pltpu.make_async_copy(x_out.at[:, at_out], b_out.at[:, at_out], sems.at[0, i]),
                pltpu.make_async_copy(w_out.at[at_out, :], v_out.at[at_out, :], sems.at[1, i]),
                pltpu.make_async_copy(x_in.at[:, at_in], b_in.at[:, at_in], sems.at[2, i]),
                pltpu.make_async_copy(w_in.at[at_in, :], v_in.at[at_in, :], sems.at[3, i]),
            ]
        )
    for group in copies:
        for copy in group:
            copy.start()
    shard = lax.axis_index("row") * n_col + lax.axis_index("col")
    base = (shard * tokens).astype(jnp.float32)
    ends = doc_ends(lens[...])
    token = lax.broadcasted_iota(jnp.int32, (1, tokens), 1).astype(jnp.float32)
    slot = docs_at(ends, token + base) - docs_at(ends, jnp.zeros((1, tokens)) + base)
    acc_in = jnp.zeros((tokens, w_in.shape[1]), jnp.float32)
    acc_out = jnp.zeros((tokens, rank_out), jnp.float32)
    for i in range(STEPS):
        at_in, at_out = pl.ds(i * k_in, k_in), pl.ds(i * k_out, k_out)
        for copy in copies[i]:
            copy.wait()
        acc_out += jnp.dot(
            b_out[:, at_out], v_out[at_out, :], preferred_element_type=jnp.float32
        )
        acc_in += jnp.dot(b_in[:, at_in], v_in[at_in, :], preferred_element_type=jnp.float32)
    low_in = acc_in.astype(jnp.bfloat16)
    low_out = acc_out.astype(jnp.bfloat16).astype(jnp.float32).T
    devices, _, rows, _ = out.shape
    for s in range(SLOTS):
        masked = jnp.where(slot == float(s), low_out, 0.0).astype(jnp.bfloat16)
        part = jnp.dot(masked, low_in, preferred_element_type=jnp.float32)
        for j in range(devices):
            out[j, s] = part[j * rows : (j + 1) * rows]


def partials_call(x_in, x_out, w_in, w_out, lens, tile, n_col, devices):
    rank_in, rank_out = w_in.shape[1], w_out.shape[1]
    far = pl.BlockSpec(memory_space=pltpu.HBM)
    return pl.pallas_call(
        functools.partial(partials_kernel, n_col),
        in_specs=[pl.BlockSpec(memory_space=pltpu.VMEM)] + [far] * 5,
        out_specs=pl.BlockSpec(memory_space=pltpu.VMEM),
        out_shape=pltpu.VMEM((devices, SLOTS, rank_out // devices, rank_in), jnp.float32),
        scratch_shapes=[
            pltpu.VMEM(x_in.shape, x_in.dtype),
            pltpu.VMEM(x_out.shape, x_out.dtype),
            pltpu.VMEM(w_in.shape, w_in.dtype),
            pltpu.VMEM(w_out.shape, w_out.dtype),
            pltpu.SemaphoreType.DMA((4, STEPS)),
        ],
        compiler_params=pltpu.CompilerParams(vmem_limit_bytes=62_495_744),
        name="partials",
    )(lens, x_in, x_out, w_in, w_out, pltpu.with_memory_space_constraint(tile, pltpu.HBM))


def pause_kernel(*refs):
    del refs


def pause_call(*after):
    return pl.pallas_call(
        pause_kernel,
        in_specs=[pl.BlockSpec(memory_space=pltpu.VMEM)] * len(after),
        out_specs=pl.BlockSpec(memory_space=pltpu.VMEM),
        out_shape=pltpu.VMEM((8, 128), jnp.float32),
        compiler_params=pltpu.CompilerParams(vmem_limit_bytes=MIB, has_side_effects=True),
        cost_estimate=pl.CostEstimate(
            flops=12_000_000_000, bytes_accessed=36_000_000, transcendentals=0
        ),
        name="pause",
    )(*after)


def combine_kernel(tokens, lens, docs_row, mark, got, out):
    del mark
    docs = lens.shape[1]
    pieces, rank = got.shape
    rows = out.shape[1] // rank
    slots = pieces // rows
    ends = doc_ends(lens[...])
    m = lax.broadcasted_iota(jnp.int32, (1, slots), 1)
    source = lax.shift_right_logical(m * 52429, 18)
    first = docs_at(ends, (source * tokens).astype(jnp.float32))
    doc = first + (m - source * SLOTS).astype(jnp.float32)
    row = lax.broadcasted_iota(jnp.int32, (docs, docs), 0)
    col = lax.broadcasted_iota(jnp.int32, (docs, docs), 1)
    wanted = jnp.broadcast_to(docs_row[...].astype(jnp.float32), (docs, docs))
    wanted = jnp.sum(jnp.where(col == row, wanted, 0.0), axis=1, keepdims=True)
    onehot = jnp.where(wanted == doc, 1.0, 0.0)
    for p in range(rows):
        piece = got[pl.ds(p, slots, stride=rows), :]
        out[:, p * rank : (p + 1) * rank] = jnp.dot(
            onehot, piece, precision=lax.Precision.HIGHEST, preferred_element_type=jnp.float32
        )


def combine_call(got, lens, docs_row, mark, tokens):
    devices, slots, rows, rank = got.shape
    docs = lens.shape[1]
    return pl.pallas_call(
        functools.partial(combine_kernel, tokens),
        out_shape=jax.ShapeDtypeStruct((docs, rows * rank), jnp.float32),
        compiler_params=pltpu.CompilerParams(vmem_limit_bytes=4 * MIB),
        name="combine",
    )(lens, docs_row, mark, got.reshape(devices * slots * rows, rank))


def split(x):
    high = x.astype(jnp.bfloat16)
    low = (x - high.astype(jnp.float32)).astype(jnp.bfloat16)
    return jnp.concatenate([high, low], axis=0)


def spread(values, place, mine, kept, given, where):
    low = 1 << place
    for at in range(len(values) // 2):
        first = (at // low) * 2 * low + at % low
        a, b = values[first], values[first + low]
        kept[at, :, where] = jnp.where(mine, b, a)
        given[at, :, where] = jnp.where(mine, a, b)


def has_bit(bit):
    return lax.rem(lax.div(lax.axis_index("row"), bit), 2) == 1


def product_kernel(at, has_first, half, bit, *refs):
    parts, refs = refs[: len(at)], refs[len(at) :]
    f_ref, outs = refs[0], refs[1 + has_first :]
    docs, size = parts[0].shape
    cols = outs[0].shape[-1]
    base = 0 if half is None else half * cols
    me = lax.axis_index("col")
    both = [split(part[...]) for part in parts]
    width = 512 if cols % 512 == 0 else cols
    for n in range(cols // width):
        where = slice(n * width, (n + 1) * width)
        source = slice(base + n * width, base + (n + 1) * width)
        total = jnp.zeros((2 * docs, width), jnp.float32)
        for k, x in zip(at, both):
            rows = pl.ds(pl.multiple_of(jnp.bitwise_xor(me, k) * size, size), size)
            tile = f_ref[rows, source].astype(jnp.bfloat16)
            total += jnp.dot(x, tile, preferred_element_type=jnp.float32)
        total = total[:docs] + total[docs:]
        if has_first:
            total += refs[1][:, source]
        if half is None:
            outs[0][:, where] = total
            continue
        groups, height, _ = outs[0].shape
        values = [total[g * height : (g + 1) * height] for g in range(2 * groups)]
        spread(values, bit.bit_length() - 1, has_bit(bit), *outs, where)


def product_call(parts, at, fisher, first, groups=None, half=None, bit=None):
    docs = parts[at[0]].shape[0]
    cols = fisher.shape[1]
    shape, count = (docs, cols), 1
    if half is not None:
        shape, count = (groups // 2, docs // groups, cols // HALVES), 2
    args = [parts[k] for k in at] + [fisher] + ([] if first is None else [first])
    return pl.pallas_call(
        functools.partial(product_kernel, at, first is not None, half, bit),
        in_specs=[pl.BlockSpec(memory_space=pltpu.VMEM)] * len(args),
        out_specs=[pl.BlockSpec(memory_space=pltpu.VMEM)] * count,
        out_shape=[jax.ShapeDtypeStruct(shape, jnp.float32)] * count,
        compiler_params=pltpu.CompilerParams(vmem_limit_bytes=12 * MIB),
    )(*args)


def fold_kernel(place, bit, mine, got, kept, given):
    values = [mine[g] + got[g] for g in range(mine.shape[0])]
    spread(values, place, has_bit(bit), kept, given, slice(None))


def fold_call(mine, got, place, bit):
    groups, height, cols = mine.shape
    return pl.pallas_call(
        functools.partial(fold_kernel, place, bit),
        in_specs=[pl.BlockSpec(memory_space=pltpu.VMEM)] * 2,
        out_specs=[pl.BlockSpec(memory_space=pltpu.VMEM)] * 2,
        out_shape=[jax.ShapeDtypeStruct((groups // 2, height, cols), jnp.float32)] * 2,
        compiler_params=pltpu.CompilerParams(vmem_limit_bytes=4 * MIB),
    )(mine, got)


def finish_kernel(*refs):
    pieces, out = refs[:-1], refs[-1]
    cols = pieces[0].shape[-1]
    for half in range(len(pieces) // 2):
        where = slice(half * cols, (half + 1) * cols)
        out[:, where] = pieces[2 * half][0] + pieces[2 * half + 1][0]


def finish_call(pieces):
    _, height, cols = pieces[0].shape
    return pl.pallas_call(
        finish_kernel,
        in_specs=[pl.BlockSpec(memory_space=pltpu.VMEM)] * len(pieces),
        out_specs=pl.BlockSpec(memory_space=pltpu.VMEM),
        out_shape=jax.ShapeDtypeStruct((height, len(pieces) // 2 * cols), jnp.float32),
        compiler_params=pltpu.CompilerParams(vmem_limit_bytes=4 * MIB),
        name="finish",
    )(*pieces)


def bit_orders(n_row):
    bits = [1 << p for p in range(n_row.bit_length() - 1)]
    return bits, [bits[1], bits[0]] + bits[2:]


def exchange(x, axis, bit):
    size = lax.axis_size(axis)
    return lax.ppermute(x, axis, [(i, i ^ bit) for i in range(size)])


def per_device(
    saved_inputs, output_grads, proj_in, proj_out, doc_lengths, device_docs, fisher_inverse
):
    tokens = saved_inputs.shape[0]
    n_row, n_col = lax.axis_size("row"), lax.axis_size("col")
    devices = n_row * n_col
    lens = doc_lengths.reshape(1, -1)
    docs_row = device_docs.reshape(1, -1)
    fisher = pltpu.with_memory_space_constraint(fisher_inverse, pltpu.VMEM)
    partials = partials_call(
        saved_inputs, output_grads, proj_in, proj_out, lens, fisher_inverse, n_col, devices
    )
    mark = pause_call(pause_call())
    got = lax.all_to_all(partials, ("row", "col"), 0, 0, tiled=True)
    mine = combine_call(got, lens, docs_row, mark, tokens)
    parts = {0: mine}
    bit = n_col // 2
    parts[bit] = exchange(mine, "col", bit)
    parts[1] = exchange(mine, "col", 1)
    while bit > 2:
        bit //= 2
        for k in [k for k in parts if k != 1]:
            parts[k ^ bit] = exchange(parts[k], "col", bit)
    evens = [k for k in parts if k > 1]
    for k in evens:
        parts[k ^ 1] = exchange(parts[k], "col", 1)
    (sums,) = product_call(parts, [0, 1], fisher, None)
    (sums,) = product_call(parts, evens, fisher, sums)
    odds = [k ^ 1 for k in evens]
    orders = bit_orders(n_row)
    held, left = [], []
    for half, bits in enumerate(orders):
        held.append(product_call(parts, odds, fisher, sums, n_row, half, bits[0]))
        left.append(sorted(set(bits) - {bits[0]}))
    pieces = []
    for stage in range(len(orders[0])):
        for half, bits in enumerate(orders):
            kept, given = held[half]
            got = exchange(given, "row", bits[stage])
            if not left[half]:
                pieces += [kept, got]
                continue
            bit = bits[stage + 1]
            place = left[half].index(bit)
            left[half].remove(bit)
            held[half] = fold_call(kept, got, place, bit)
    return finish_call(pieces)


def solution(mesh):
    placed = (P(("row", "col"), None), P(("row", "col"), None), P(), P(), P(), P(), P("row", "col"))
    return jax.shard_map(
        per_device, mesh=mesh, in_specs=placed, out_specs=P("row", "col"), check_vma=False
    )
```

```python
import functools

import jax
import jax.numpy as jnp
from jax import lax
from jax.experimental import pallas as pl
from jax.experimental.pallas import tpu as pltpu
from jax.sharding import PartitionSpec as P


SLOTS = 5
STEPS = 8
QUAD = 4
TURNS = (1, 2, 3)
MIB = 1024 * 1024


def doc_ends(lens):
    docs = lens.shape[1]
    row = lax.broadcasted_iota(jnp.int32, (docs, docs), 0)
    col = lax.broadcasted_iota(jnp.int32, (docs, docs), 1)
    wide = jnp.broadcast_to(lens.astype(jnp.float32), (docs, docs))
    return jnp.sum(jnp.where(col <= row, wide, 0.0), axis=1, keepdims=True)


def docs_at(ends, positions):
    return jnp.sum(jnp.where(ends <= positions, 1.0, 0.0), axis=0, keepdims=True)


def partials_kernel(
    n_col, lens, x_in, x_out, w_in, w_out, tile, out, b_in, b_out, v_in, v_out, sems
):
    del tile
    tokens, rank_out = b_out.shape[0], w_out.shape[1]
    k_in, k_out = x_in.shape[1] // STEPS, x_out.shape[1] // STEPS
    copies = []
    for i in range(STEPS):
        at_in, at_out = pl.ds(i * k_in, k_in), pl.ds(i * k_out, k_out)
        copies.append(
            [
                pltpu.make_async_copy(x_out.at[:, at_out], b_out.at[:, at_out], sems.at[0, i]),
                pltpu.make_async_copy(w_out.at[at_out, :], v_out.at[at_out, :], sems.at[1, i]),
                pltpu.make_async_copy(x_in.at[:, at_in], b_in.at[:, at_in], sems.at[2, i]),
                pltpu.make_async_copy(w_in.at[at_in, :], v_in.at[at_in, :], sems.at[3, i]),
            ]
        )
    for group in copies:
        for copy in group:
            copy.start()
    shard = lax.axis_index("row") * n_col + lax.axis_index("col")
    base = (shard * tokens).astype(jnp.float32)
    ends = doc_ends(lens[...])
    token = lax.broadcasted_iota(jnp.int32, (1, tokens), 1).astype(jnp.float32)
    slot = docs_at(ends, token + base) - docs_at(ends, jnp.zeros((1, tokens)) + base)
    acc_in = jnp.zeros((tokens, w_in.shape[1]), jnp.float32)
    acc_out = jnp.zeros((tokens, rank_out), jnp.float32)
    for i in range(STEPS):
        at_in, at_out = pl.ds(i * k_in, k_in), pl.ds(i * k_out, k_out)
        for copy in copies[i]:
            copy.wait()
        acc_out += jnp.dot(
            b_out[:, at_out], v_out[at_out, :], preferred_element_type=jnp.float32
        )
        acc_in += jnp.dot(b_in[:, at_in], v_in[at_in, :], preferred_element_type=jnp.float32)
    low_in = acc_in.astype(jnp.bfloat16)
    low_out = acc_out.astype(jnp.bfloat16).astype(jnp.float32).T
    devices, _, rows, _ = out.shape
    for s in range(SLOTS):
        masked = jnp.where(slot == float(s), low_out, 0.0).astype(jnp.bfloat16)
        part = jnp.dot(masked, low_in, preferred_element_type=jnp.float32)
        for j in range(devices):
            out[j, s] = part[j * rows : (j + 1) * rows]


def partials_call(x_in, x_out, w_in, w_out, lens, tile, n_col, devices):
    rank_in, rank_out = w_in.shape[1], w_out.shape[1]
    far = pl.BlockSpec(memory_space=pltpu.HBM)
    return pl.pallas_call(
        functools.partial(partials_kernel, n_col),
        in_specs=[pl.BlockSpec(memory_space=pltpu.VMEM)] + [far] * 5,
        out_specs=pl.BlockSpec(memory_space=pltpu.VMEM),
        out_shape=pltpu.VMEM((devices, SLOTS, rank_out // devices, rank_in), jnp.float32),
        scratch_shapes=[
            pltpu.VMEM(x_in.shape, x_in.dtype),
            pltpu.VMEM(x_out.shape, x_out.dtype),
            pltpu.VMEM(w_in.shape, w_in.dtype),
            pltpu.VMEM(w_out.shape, w_out.dtype),
            pltpu.SemaphoreType.DMA((4, STEPS)),
        ],
        compiler_params=pltpu.CompilerParams(vmem_limit_bytes=62_495_744),
        name="partials",
    )(lens, x_in, x_out, w_in, w_out, pltpu.with_memory_space_constraint(tile, pltpu.HBM))


def pause_kernel(*refs):
    del refs


def pause_call(*after):
    return pl.pallas_call(
        pause_kernel,
        in_specs=[pl.BlockSpec(memory_space=pltpu.VMEM)] * len(after),
        out_specs=pl.BlockSpec(memory_space=pltpu.VMEM),
        out_shape=pltpu.VMEM((8, 128), jnp.float32),
        compiler_params=pltpu.CompilerParams(vmem_limit_bytes=MIB, has_side_effects=True),
        cost_estimate=pl.CostEstimate(
            flops=12_000_000_000, bytes_accessed=36_000_000, transcendentals=0
        ),
        name="pause",
    )(*after)


def combine_kernel(tokens, lens, docs_row, mark, got, out):
    del mark
    docs = lens.shape[1]
    pieces, rank = got.shape
    rows = out.shape[1] // rank
    slots = pieces // rows
    ends = doc_ends(lens[...])
    m = lax.broadcasted_iota(jnp.int32, (1, slots), 1)
    source = lax.shift_right_logical(m * 52429, 18)
    first = docs_at(ends, (source * tokens).astype(jnp.float32))
    doc = first + (m - source * SLOTS).astype(jnp.float32)
    row = lax.broadcasted_iota(jnp.int32, (docs, docs), 0)
    col = lax.broadcasted_iota(jnp.int32, (docs, docs), 1)
    wanted = jnp.broadcast_to(docs_row[...].astype(jnp.float32), (docs, docs))
    wanted = jnp.sum(jnp.where(col == row, wanted, 0.0), axis=1, keepdims=True)
    onehot = jnp.where(wanted == doc, 1.0, 0.0)
    for p in range(rows):
        piece = got[pl.ds(p, slots, stride=rows), :]
        out[:, p * rank : (p + 1) * rank] = jnp.dot(
            onehot, piece, precision=lax.Precision.HIGHEST, preferred_element_type=jnp.float32
        )


def combine_call(got, lens, docs_row, mark, tokens):
    devices, slots, rows, rank = got.shape
    docs = lens.shape[1]
    return pl.pallas_call(
        functools.partial(combine_kernel, tokens),
        out_shape=jax.ShapeDtypeStruct((docs, rows * rank), jnp.float32),
        compiler_params=pltpu.CompilerParams(vmem_limit_bytes=4 * MIB),
        name="combine",
    )(lens, docs_row, mark, got.reshape(devices * slots * rows, rank))


def split(x):
    high = x.astype(jnp.bfloat16)
    low = (x - high.astype(jnp.float32)).astype(jnp.bfloat16)
    return jnp.concatenate([high, low], axis=0)


def product_kernel(at, has_first, *refs):
    parts, refs = refs[: len(at)], refs[len(at) :]
    f_ref, outs = refs[0], refs[1 + has_first :]
    docs, size = parts[0].shape
    cols = f_ref.shape[1]
    me = lax.axis_index("col")
    both = [split(part[...]) for part in parts]
    width = 512 if cols % 512 == 0 else cols
    for n in range(cols // width):
        where = slice(n * width, (n + 1) * width)
        total = jnp.zeros((2 * docs, width), jnp.float32)
        for k, x in zip(at, both):
            rows = pl.ds(pl.multiple_of(jnp.bitwise_xor(me, k) * size, size), size)
            tile = f_ref[rows, where].astype(jnp.bfloat16)
            total += jnp.dot(x, tile, preferred_element_type=jnp.float32)
        total = total[:docs] + total[docs:]
        if has_first:
            total += refs[1][:, where]
        if len(outs) == 1:
            outs[0][:, where] = total
            continue
        groups, height, _ = outs[-1].shape
        for g in range(groups):
            outs[-1][g, :, where] = total[g * height : (g + 1) * height]
    if len(outs) > 1:
        cross, own, held = outs[:QUAD], outs[QUAD:-1], outs[-1]
        row = lax.axis_index("row")
        for k in range(QUAD):
            own[k][...] = held[jnp.bitwise_xor(row, k)]
            for t in range(1, held.shape[0] // QUAD):
                cross[k][t - 1] = held[jnp.bitwise_xor(row, QUAD * t + k)]


def product_call(parts, at, fisher, first, groups=None):
    docs = parts[at[0]].shape[0]
    cols = fisher.shape[1]
    shapes, scratch = [(docs, cols)], []
    if groups is not None:
        height = docs // groups
        shapes = [(groups // QUAD - 1, height, cols)] * QUAD + [(height, cols)] * QUAD
        scratch = [pltpu.VMEM((groups, height, cols), jnp.float32)]
    args = [parts[k] for k in at] + [fisher] + ([] if first is None else [first])
    return pl.pallas_call(
        functools.partial(product_kernel, at, first is not None),
        in_specs=[pl.BlockSpec(memory_space=pltpu.VMEM)] * len(args),
        out_specs=[pl.BlockSpec(memory_space=pltpu.VMEM)] * len(shapes),
        out_shape=[jax.ShapeDtypeStruct(shape, jnp.float32) for shape in shapes],
        scratch_shapes=scratch,
        compiler_params=pltpu.CompilerParams(vmem_limit_bytes=12 * MIB),
    )(*args)


def fold_kernel(*refs):
    pieces, outs = refs[:QUAD], refs[QUAD:]
    for t, out in enumerate(outs):
        out[...] = (pieces[0][t] + pieces[1][t]) + (pieces[2][t] + pieces[3][t])


def fold_call(pieces):
    others, height, cols = pieces[0].shape
    return pl.pallas_call(
        fold_kernel,
        in_specs=[pl.BlockSpec(memory_space=pltpu.VMEM)] * QUAD,
        out_specs=[pl.BlockSpec(memory_space=pltpu.VMEM)] * others,
        out_shape=[jax.ShapeDtypeStruct((height, cols), jnp.float32)] * others,
        compiler_params=pltpu.CompilerParams(vmem_limit_bytes=4 * MIB),
        name="fold",
    )(*pieces)


def finish_kernel(*refs):
    total = refs[0][...]
    for piece in refs[1:-1]:
        total += piece[...]
    refs[-1][...] = total


def finish_call(pieces):
    return pl.pallas_call(
        finish_kernel,
        in_specs=[pl.BlockSpec(memory_space=pltpu.VMEM)] * len(pieces),
        out_specs=pl.BlockSpec(memory_space=pltpu.VMEM),
        out_shape=jax.ShapeDtypeStruct(pieces[0].shape, jnp.float32),
        compiler_params=pltpu.CompilerParams(vmem_limit_bytes=4 * MIB),
        name="finish",
    )(*pieces)


def exchange(x, axis, bit):
    size = lax.axis_size(axis)
    return lax.ppermute(x, axis, [(i, i ^ bit) for i in range(size)])


def per_device(
    saved_inputs, output_grads, proj_in, proj_out, doc_lengths, device_docs, fisher_inverse
):
    tokens = saved_inputs.shape[0]
    n_row, n_col = lax.axis_size("row"), lax.axis_size("col")
    devices = n_row * n_col
    lens = doc_lengths.reshape(1, -1)
    docs_row = device_docs.reshape(1, -1)
    fisher = pltpu.with_memory_space_constraint(fisher_inverse, pltpu.VMEM)
    partials = partials_call(
        saved_inputs, output_grads, proj_in, proj_out, lens, fisher_inverse, n_col, devices
    )
    mark = pause_call(pause_call())
    got = lax.all_to_all(partials, ("row", "col"), 0, 0, tiled=True)
    mine = combine_call(got, lens, docs_row, mark, tokens)
    parts = {0: mine}
    bit = n_col // 2
    parts[bit] = exchange(mine, "col", bit)
    parts[1] = exchange(mine, "col", 1)
    while bit > 2:
        bit //= 2
        for k in [k for k in parts if k != 1]:
            parts[k ^ bit] = exchange(parts[k], "col", bit)
    evens = [k for k in parts if k > 1]
    for k in evens:
        parts[k ^ 1] = exchange(parts[k], "col", 1)
    (sums,) = product_call(parts, [0, 1], fisher, None)
    (sums,) = product_call(parts, evens, fisher, sums)
    odds = [k ^ 1 for k in evens]
    results = product_call(parts, odds, fisher, sums, n_row)
    cross, own = list(results[:QUAD]), list(results[QUAD:])
    for k in TURNS:
        cross[k] = exchange(cross[k], "row", k)
    for k in TURNS:
        own[k] = exchange(own[k], "row", k)
    far = fold_call(cross)
    for t, piece in enumerate(far):
        own.append(exchange(piece, "row", QUAD * (t + 1)))
    return finish_call(own)


def solution(mesh):
    placed = (P(("row", "col"), None), P(("row", "col"), None), P(), P(), P(), P(), P("row", "col"))
    return jax.shard_map(
        per_device, mesh=mesh, in_specs=placed, out_specs=P("row", "col"), check_vma=False
    )
```

```python
import functools

import jax
import jax.numpy as jnp
from jax import lax
from jax.experimental import pallas as pl
from jax.experimental.pallas import tpu as pltpu
from jax.sharding import PartitionSpec as P


SLOTS = 5
CUTS = (0.07, 0.19, 0.32, 0.46, 0.6, 0.74, 0.87, 1.0)
QUAD = 4
TURNS = (1, 2, 3)
MIB = 1024 * 1024


def doc_ends(lens):
    docs = lens.shape[1]
    row = lax.broadcasted_iota(jnp.int32, (docs, docs), 0)
    col = lax.broadcasted_iota(jnp.int32, (docs, docs), 1)
    wide = jnp.broadcast_to(lens.astype(jnp.float32), (docs, docs))
    return jnp.sum(jnp.where(col <= row, wide, 0.0), axis=1, keepdims=True)


def docs_at(ends, positions):
    return jnp.sum(jnp.where(ends <= positions, 1.0, 0.0), axis=0, keepdims=True)


def chunks(size):
    unit = 256 if size % 256 == 0 else 128
    ends = [int(round(cut * size / unit)) * unit for cut in CUTS]
    return [pl.ds(a, b - a) if b > a else None for a, b in zip([0] + ends, ends)]


def slot_table(lens, docs_row, devices, tokens):
    docs = lens.shape[1]
    ends = doc_ends(lens)
    m = lax.broadcasted_iota(jnp.int32, (1, devices * SLOTS), 1)
    source = lax.shift_right_logical(m * 52429, 18)
    first = docs_at(ends, (source * tokens).astype(jnp.float32))
    doc = first + (m - source * SLOTS).astype(jnp.float32)
    row = lax.broadcasted_iota(jnp.int32, (docs, docs), 0)
    col = lax.broadcasted_iota(jnp.int32, (docs, docs), 1)
    wanted = jnp.broadcast_to(docs_row.astype(jnp.float32), (docs, docs))
    wanted = jnp.sum(jnp.where(col == row, wanted, 0.0), axis=1, keepdims=True)
    return jnp.where(wanted == doc, 1.0, 0.0)


def partials_kernel(
    n_col,
    lens,
    docs_row,
    x_in,
    x_out,
    w_in,
    w_out,
    tile,
    out,
    table,
    b_in,
    b_out,
    v_in,
    v_out,
    sems,
):
    del tile
    tokens, rank_out = b_out.shape[0], w_out.shape[1]
    copies = []
    steps = list(zip(chunks(x_out.shape[1]), chunks(x_in.shape[1])))
    for i, (at_out, at_in) in enumerate(steps):
        copies.append([])
        if at_out is not None:
            copies[-1] += [
                pltpu.make_async_copy(x_out.at[:, at_out], b_out.at[:, at_out], sems.at[0, i]),
                pltpu.make_async_copy(w_out.at[at_out, :], v_out.at[at_out, :], sems.at[1, i]),
            ]
        if at_in is not None:
            copies[-1] += [
                pltpu.make_async_copy(x_in.at[:, at_in], b_in.at[:, at_in], sems.at[2, i]),
                pltpu.make_async_copy(w_in.at[at_in, :], v_in.at[at_in, :], sems.at[3, i]),
            ]
    for group in copies:
        for copy in group:
            copy.start()
    shard = lax.axis_index("row") * n_col + lax.axis_index("col")
    base = (shard * tokens).astype(jnp.float32)
    ends = doc_ends(lens[...])
    token = lax.broadcasted_iota(jnp.int32, (1, tokens), 1).astype(jnp.float32)
    slot = docs_at(ends, token + base) - docs_at(ends, jnp.zeros((1, tokens)) + base)
    table[...] = slot_table(lens[...], docs_row[...], out.shape[0], tokens)
    acc_in = jnp.zeros((tokens, w_in.shape[1]), jnp.float32)
    acc_out = jnp.zeros((tokens, rank_out), jnp.float32)
    for group, (at_out, at_in) in zip(copies, steps):
        for copy in group:
            copy.wait()
        if at_out is not None:
            acc_out += jnp.dot(
                b_out[:, at_out], v_out[at_out, :], preferred_element_type=jnp.float32
            )
        if at_in is not None:
            acc_in += jnp.dot(
                b_in[:, at_in], v_in[at_in, :], preferred_element_type=jnp.float32
            )
    low_in = acc_in.astype(jnp.bfloat16)
    low_out = acc_out.astype(jnp.bfloat16).astype(jnp.float32).T
    devices, _, rows, _ = out.shape
    for s in range(SLOTS):
        masked = jnp.where(slot == float(s), low_out, 0.0).astype(jnp.bfloat16)
        part = jnp.dot(masked, low_in, preferred_element_type=jnp.float32)
        for j in range(devices):
            out[j, s] = part[j * rows : (j + 1) * rows]


def partials_call(x_in, x_out, w_in, w_out, lens, docs_row, tile, n_col, devices):
    rank_in, rank_out = w_in.shape[1], w_out.shape[1]
    far, near = pl.BlockSpec(memory_space=pltpu.HBM), pl.BlockSpec(memory_space=pltpu.VMEM)
    return pl.pallas_call(
        functools.partial(partials_kernel, n_col),
        in_specs=[near, near] + [far] * 5,
        out_specs=[near, near],
        out_shape=[
            pltpu.VMEM((devices, SLOTS, rank_out // devices, rank_in), jnp.float32),
            pltpu.VMEM((docs_row.shape[1], devices * SLOTS), jnp.float32),
        ],
        scratch_shapes=[
            pltpu.VMEM(x_in.shape, x_in.dtype),
            pltpu.VMEM(x_out.shape, x_out.dtype),
            pltpu.VMEM(w_in.shape, w_in.dtype),
            pltpu.VMEM(w_out.shape, w_out.dtype),
            pltpu.SemaphoreType.DMA((4, len(CUTS))),
        ],
        compiler_params=pltpu.CompilerParams(vmem_limit_bytes=62_495_744),
        name="partials",
    )(lens, docs_row, x_in, x_out, w_in, w_out, pltpu.with_memory_space_constraint(tile, pltpu.HBM))


def pause_kernel(*refs):
    del refs


def pause_call(*after):
    return pl.pallas_call(
        pause_kernel,
        in_specs=[pl.BlockSpec(memory_space=pltpu.VMEM)] * len(after),
        out_specs=pl.BlockSpec(memory_space=pltpu.VMEM),
        out_shape=pltpu.VMEM((8, 128), jnp.float32),
        compiler_params=pltpu.CompilerParams(vmem_limit_bytes=MIB, has_side_effects=True),
        cost_estimate=pl.CostEstimate(
            flops=12_000_000_000, bytes_accessed=36_000_000, transcendentals=0
        ),
        name="pause",
    )(*after)


def combine_kernel(mark, table, got, out):
    del mark
    slots = table.shape[1]
    rank = got.shape[1]
    rows = got.shape[0] // slots
    pieces = []
    for p in range(rows):
        rest = got[pl.ds(p, slots, stride=rows), :]
        for _ in range(3):
            pieces.append(rest.astype(jnp.bfloat16))
            rest = rest - pieces[-1].astype(jnp.float32)
    sums = jnp.dot(
        table[...].astype(jnp.bfloat16),
        jnp.concatenate(pieces, axis=1),
        preferred_element_type=jnp.float32,
    )
    for p in range(rows):
        a, b, c = (sums[:, (3 * p + i) * rank : (3 * p + i + 1) * rank] for i in range(3))
        out[:, p * rank : (p + 1) * rank] = a + (b + c)


def combine_call(got, table, mark):
    devices, slots, rows, rank = got.shape
    return pl.pallas_call(
        combine_kernel,
        out_shape=jax.ShapeDtypeStruct((table.shape[0], rows * rank), jnp.float32),
        compiler_params=pltpu.CompilerParams(vmem_limit_bytes=4 * MIB),
        name="combine",
    )(mark, table, got.reshape(devices * slots * rows, rank))


def split(x):
    high = x.astype(jnp.bfloat16)
    low = (x - high.astype(jnp.float32)).astype(jnp.bfloat16)
    return jnp.concatenate([high, low], axis=0)


def product_kernel(at, has_first, *refs):
    parts, refs = refs[: len(at)], refs[len(at) :]
    f_ref, outs = refs[0], refs[1 + has_first :]
    docs, size = parts[0].shape
    cols = f_ref.shape[1]
    me = lax.axis_index("col")
    both = [split(part[...]) for part in parts]
    width = 512 if cols % 512 == 0 else cols
    for n in range(cols // width):
        where = slice(n * width, (n + 1) * width)
        total = jnp.zeros((2 * docs, width), jnp.float32)
        for k, x in zip(at, both):
            rows = pl.ds(pl.multiple_of(jnp.bitwise_xor(me, k) * size, size), size)
            tile = f_ref[rows, where].astype(jnp.bfloat16)
            total += jnp.dot(x, tile, preferred_element_type=jnp.float32)
        total = total[:docs] + total[docs:]
        if has_first:
            total += refs[1][:, where]
        if len(outs) == 1:
            outs[0][:, where] = total
            continue
        groups, height, _ = outs[-1].shape
        for g in range(groups):
            outs[-1][g, :, where] = total[g * height : (g + 1) * height]
    if len(outs) > 1:
        cross, own, held = outs[:QUAD], outs[QUAD:-1], outs[-1]
        row = lax.axis_index("row")
        for k in range(QUAD):
            own[k][...] = held[jnp.bitwise_xor(row, k)]
            for t in range(1, held.shape[0] // QUAD):
                cross[k][t - 1] = held[jnp.bitwise_xor(row, QUAD * t + k)]


def product_call(parts, at, fisher, first, groups=None):
    docs = parts[at[0]].shape[0]
    cols = fisher.shape[1]
    shapes, scratch = [(docs, cols)], []
    if groups is not None:
        height = docs // groups
        shapes = [(groups // QUAD - 1, height, cols)] * QUAD + [(height, cols)] * QUAD
        scratch = [pltpu.VMEM((groups, height, cols), jnp.float32)]
    args = [parts[k] for k in at] + [fisher] + ([] if first is None else [first])
    return pl.pallas_call(
        functools.partial(product_kernel, at, first is not None),
        in_specs=[pl.BlockSpec(memory_space=pltpu.VMEM)] * len(args),
        out_specs=[pl.BlockSpec(memory_space=pltpu.VMEM)] * len(shapes),
        out_shape=[jax.ShapeDtypeStruct(shape, jnp.float32) for shape in shapes],
        scratch_shapes=scratch,
        compiler_params=pltpu.CompilerParams(vmem_limit_bytes=12 * MIB),
    )(*args)


def fold_kernel(*refs):
    pieces, outs = refs[:QUAD], refs[QUAD:]
    for t, out in enumerate(outs):
        out[...] = (pieces[0][t] + pieces[1][t]) + (pieces[2][t] + pieces[3][t])


def fold_call(pieces):
    others, height, cols = pieces[0].shape
    return pl.pallas_call(
        fold_kernel,
        in_specs=[pl.BlockSpec(memory_space=pltpu.VMEM)] * QUAD,
        out_specs=[pl.BlockSpec(memory_space=pltpu.VMEM)] * others,
        out_shape=[jax.ShapeDtypeStruct((height, cols), jnp.float32)] * others,
        compiler_params=pltpu.CompilerParams(vmem_limit_bytes=4 * MIB),
        name="fold",
    )(*pieces)


def finish_kernel(*refs):
    total = refs[0][...]
    for piece in refs[1:-1]:
        total += piece[...]
    refs[-1][...] = total


def finish_call(pieces):
    return pl.pallas_call(
        finish_kernel,
        in_specs=[pl.BlockSpec(memory_space=pltpu.VMEM)] * len(pieces),
        out_specs=pl.BlockSpec(memory_space=pltpu.VMEM),
        out_shape=jax.ShapeDtypeStruct(pieces[0].shape, jnp.float32),
        compiler_params=pltpu.CompilerParams(vmem_limit_bytes=4 * MIB),
        name="finish",
    )(*pieces)


def exchange(x, axis, bit):
    size = lax.axis_size(axis)
    return lax.ppermute(x, axis, [(i, i ^ bit) for i in range(size)])


def per_device(
    saved_inputs, output_grads, proj_in, proj_out, doc_lengths, device_docs, fisher_inverse
):
    n_row, n_col = lax.axis_size("row"), lax.axis_size("col")
    devices = n_row * n_col
    lens = doc_lengths.reshape(1, -1)
    docs_row = device_docs.reshape(1, -1)
    fisher = pltpu.with_memory_space_constraint(fisher_inverse, pltpu.VMEM)
    partials, table = partials_call(
        saved_inputs,
        output_grads,
        proj_in,
        proj_out,
        lens,
        docs_row,
        fisher_inverse,
        n_col,
        devices,
    )
    mark = pause_call(pause_call())
    got = lax.all_to_all(partials, ("row", "col"), 0, 0, tiled=True)
    mine = combine_call(got, table, mark)
    parts = {0: mine}
    bit = n_col // 2
    parts[bit] = exchange(mine, "col", bit)
    parts[1] = exchange(mine, "col", 1)
    while bit > 2:
        bit //= 2
        for k in [k for k in parts if k != 1]:
            parts[k ^ bit] = exchange(parts[k], "col", bit)
    evens = [k for k in parts if k > 1]
    for k in evens:
        parts[k ^ 1] = exchange(parts[k], "col", 1)
    (sums,) = product_call(parts, [0, 1], fisher, None)
    (sums,) = product_call(parts, evens, fisher, sums)
    odds = [k ^ 1 for k in evens]
    results = product_call(parts, odds, fisher, sums, n_row)
    cross, own = list(results[:QUAD]), list(results[QUAD:])
    for k in TURNS:
        cross[k] = exchange(cross[k], "row", k)
    for k in TURNS:
        own[k] = exchange(own[k], "row", k)
    far = fold_call(cross)
    for t, piece in enumerate(far):
        own.append(exchange(piece, "row", QUAD * (t + 1)))
    return finish_call(own)


def solution(mesh):
    placed = (P(("row", "col"), None), P(("row", "col"), None), P(), P(), P(), P(), P("row", "col"))
    return jax.shard_map(
        per_device, mesh=mesh, in_specs=placed, out_specs=P("row", "col"), check_vma=False
    )
```
